256 devices in a mesh: seg: 16 (over z, core), head: 16 (over x, y).
Axes of the slice: x: 4, y: 4, z: 8, core: 2. Of those that a mesh axis runs over, the one named last changes fastest.
Arguments:
- inputs: bfloat16 [16, 256, 16384], P('seg', None, 'head'), may hold values from -6 to 6
- deltas: float32 [16, 256, 256], P('seg', 'head'), may hold values from 0.01 to 0.1
- rates: float32 [256], P('head'), may hold values from 0.001 to 2
- skips: float32 [256], P('head'), may hold values from 0.5 to 1.5
- writer: bfloat16 [16, 256, 1024], P('seg'), may hold values from -1.796875 to 1.796875
- reader: bfloat16 [16, 256, 1024], P('seg'), may hold values from -1.796875 to 1.796875
- grad_out: bfloat16 [16, 256, 16384], P('seg', None, 'head'), may hold values from -6 to 6
- parents: int32 [16], replicated, may hold values from -1 to 15, as said below
- levels: int32 [16], replicated, may hold values from 0 to 2, as said below
Outputs:
- outputs: bfloat16 [16, 256, 16384], P('seg', None, 'head')
- grad_inputs: bfloat16 [16, 256, 16384], P('seg', None, 'head')
- grad_deltas: float32 [16, 256, 256], P('seg', 'head')
- grad_writer: bfloat16 [16, 256, 1024], P('seg', 'head')
- grad_reader: bfloat16 [16, 256, 1024], P('seg', 'head')
The draws below stay inside these ranges and needn't reach their ends.
Inputs may be any that keep to these rules, and one draw needn't show every extreme that they name: `parents`: roots have parent -1 and level 0; every other segment's parent has a level one less than its own. A segment has at most four children, and some segment has level 2. levels[s] is the number of ancestors of segment s.
All inputs are finite; a program needn't handle non-finite values.
Results may differ from the reference program's by a relative error of at most 0.0046.
Values may be sent and summed in bfloat16 or wider, within the bound.
A program may use at most 128 MiB of HBM per device.

```python
import math
import jax
import jax.numpy as jnp
from jax import lax

H = 256
P_SIZE = 64
N = 128
G = 8
SEG_LEN = 256
BLOCK = 256
DEPTH = 3
SEGS = 16


def tree_tables(key):
    counts = jax.random.randint(jax.random.fold_in(key, 11), (SEGS,), 2, 5).astype(jnp.int32)
    shuffled = jax.random.permutation(jax.random.fold_in(key, 12), SEGS).astype(jnp.int32)
    slots = jnp.arange(SEGS, dtype=jnp.int32)
    top_place = jnp.argmax((shuffled == SEGS - 1).astype(jnp.int32)).astype(jnp.int32)
    first_value = shuffled[0]
    order = shuffled.at[top_place].set(first_value).at[0].set(SEGS - 1)

    def place(number, carry):
        parent_bfs, level_bfs, current, remain = carry
        lowest = jnp.where(remain > 0, current, current + 1)
        usable = (slots >= lowest) & (slots < number) & (level_bfs < DEPTH - 1)
        picked = jnp.min(jnp.where(usable, slots, SEGS))
        found = picked < SEGS
        safe_pick = jnp.minimum(picked, SEGS - 1)
        same = picked == current
        new_remain = jnp.where(same, remain - 1, counts[safe_pick] - 1)
        new_current = jnp.where(same, current, safe_pick)
        parent_bfs = parent_bfs.at[number].set(jnp.where(found, safe_pick, -1))
        level_bfs = level_bfs.at[number].set(jnp.where(found, level_bfs[safe_pick] + 1, 0))
        current = jnp.where(found, new_current, current)
        remain = jnp.where(found, new_remain, remain)
        return (parent_bfs, level_bfs, current, remain)
    start_carry = (jnp.full((SEGS,), -1, jnp.int32), jnp.zeros((SEGS,), jnp.int32), jnp.int32(0), counts[0])
    parent_bfs, level_bfs, current, remain = lax.fori_loop(1, SEGS, place, start_carry)
    mapped = jnp.where(parent_bfs >= 0, order[jnp.maximum(parent_bfs, 0)], -1).astype(jnp.int32)
    parent_slot = jnp.zeros((SEGS,), jnp.int32).at[order].set(mapped)
    level_slot = jnp.zeros((SEGS,), jnp.int32).at[order].set(level_bfs)
    return (parent_slot, level_slot)


def draw_parents(key, part):
    return tree_tables(key)[0]


def draw_levels(key, part):
    return tree_tables(key)[1]


def shard_levels(own_key, shape, split, smallest, high):
    def one(axis_at, parts):
        draws = jax.random.uniform(jax.random.fold_in(jax.random.fold_in(own_key, 6), axis_at), (parts,), jnp.float32, smallest / len(split), high / len(split))
        return jnp.repeat(jnp.exp(draws), shape[axis_at] // parts).reshape((-1,) + (1,) * (len(shape) - axis_at - 1))

    loudness = one(*split[0])
    for cut in split[1:]:
        loudness = loudness * one(*cut)
    return loudness


def normal_values(stream_key, extent, deviation, limit, pieces=(), kind=jnp.bfloat16):
    factor_of = shard_levels(stream_key, extent, pieces, -0.22, 0.18) if pieces else 1.0
    drawn = jax.random.normal(stream_key, extent, jnp.float32) * deviation * factor_of
    return jnp.minimum(jnp.maximum(drawn, -limit), limit).astype(kind)


def setup_inputs(seed: int = 0) -> dict:
    splits = jax.random.split(jax.random.key(seed), 10)
    inputs = normal_values(splits[0], (SEGS, SEG_LEN, H * P_SIZE), 1.0, 6.0, ((0, 16), (2, 16)))
    deltas = jnp.clip(jnp.exp(math.log(0.1) - 2.3025851 * jax.random.uniform(splits[1], (SEGS, H, SEG_LEN), jnp.float32) ** shard_levels(splits[1], (SEGS, H, SEG_LEN), ((0, 16), (1, 16)), -0.2, 0.2)), 0.01, 0.1)
    rates = jnp.clip(jnp.exp(math.log(2.0) - 7.6009024 * jax.random.uniform(splits[2], (H,), jnp.float32) ** shard_levels(splits[2], (H,), ((0, 16),), -0.2, 0.2)), 0.001, 2.0)
    skips = jnp.clip(0.5 + 1.0 * jax.random.uniform(splits[3], (H,), jnp.float32) ** shard_levels(splits[3], (H,), ((0, 16),), -0.2, 0.2), 0.5, 1.5)
    writer = normal_values(splits[4], (SEGS, SEG_LEN, G * N), 0.3, 1.796875, ((0, 16),))
    reader = normal_values(splits[5], (SEGS, SEG_LEN, G * N), 0.3, 1.796875, ((0, 16),))
    grad_out = normal_values(splits[6], (SEGS, SEG_LEN, H * P_SIZE), 1.0, 6.0, ((0, 16), (2, 16)))
    parents = draw_parents(jax.random.fold_in(splits[9], 71), 0)
    levels = draw_levels(jax.random.fold_in(splits[9], 71), 0)
    return {"inputs": inputs, "deltas": deltas, "rates": rates, "skips": skips, "writer": writer, "reader": reader, "grad_out": grad_out, "parents": parents, "levels": levels}


exact_mode = lax.Precision.HIGHEST

def round_half(values):
    return lax.optimization_barrier(values.astype(jnp.bfloat16)).astype(jnp.float32)

def ssd_forward(values, deltas, rates, writer, reader, start, block):
    length, groups, per_group, width = values.shape
    state_size = writer.shape[-1]
    blocks = length // block
    log_decay = (-rates[:, :, None] * deltas).reshape(groups, per_group, blocks, block)
    within = jnp.cumsum(log_decay, axis=-1)
    value_blk = values.reshape(blocks, block, groups, per_group, width)
    write_blk = writer.reshape(blocks, block, groups, state_size)
    read_blk = reader.reshape(blocks, block, groups, state_size)
    delta_blk = deltas.reshape(groups, per_group, blocks, block)
    scores = jnp.einsum('cign,cjgn->gcij', read_blk, write_blk, precision=exact_mode)
    positions = jnp.arange(block)
    causal = positions[:, None] >= positions[None, :]
    log_gap = within[..., :, None] - within[..., None, :]
    decays = jnp.exp(jnp.where(causal, log_gap, -jnp.inf))
    weights = scores[:, None] * decays * delta_blk[..., None, :]
    within_out = jnp.einsum('ghcij,cjghp->cighp', weights, value_blk, precision=exact_mode)
    tail_decay = jnp.exp(within[..., -1:] - within) * delta_blk
    local_state = jnp.einsum('ghcj,cjghp,cjgn->cghpn', tail_decay, value_blk, write_blk, precision=exact_mode)
    totals = jnp.exp(within[..., -1])
    current = start
    outer_terms = []
    for number in range(blocks):
        read_out = jnp.einsum('ign,ghpn->ighp', read_blk[number], current, precision=exact_mode)
        scale_in = jnp.transpose(jnp.exp(within[:, :, number, :]), (2, 0, 1))
        outer_terms.append(read_out * scale_in[..., None])
        current = totals[:, :, number, None, None] * current + local_state[number]
    output = within_out + jnp.stack(outer_terms)
    return (output.reshape(length, groups, per_group, width), current)

def segment_end(values, deltas, rates, writer):
    running = jnp.cumsum(-rates[:, :, None] * deltas, axis=-1)
    total = running[..., -1]
    tail_decay = jnp.exp(total[..., None] - running) * deltas
    local_state = jnp.einsum('ghj,jghp,jgn->ghpn', tail_decay, values, writer, precision=exact_mode)
    return (local_state, jnp.exp(total))

def start_grad(grads, deltas, rates, reader):
    running = jnp.cumsum(-rates[:, :, None] * deltas, axis=-1)
    return jnp.einsum('ghi,ighp,ign->ghpn', jnp.exp(running), grads, reader, precision=exact_mode)

def reference(inputs, deltas, rates, skips, writer, reader, grad_out, parents, levels):
    per_group = H // G
    segments = inputs.shape[0]
    length = inputs.shape[1]
    rate_grid = rates.reshape(G, per_group)
    skip_grid = skips.reshape(G, per_group)

    def unpack(number):
        values = inputs[number].astype(jnp.float32).reshape(length, G, per_group, P_SIZE)
        delta_one = deltas[number].reshape(G, per_group, length)
        write_one = writer[number].astype(jnp.float32).reshape(length, G, N)
        read_one = reader[number].astype(jnp.float32).reshape(length, G, N)
        grads = grad_out[number].astype(jnp.float32).reshape(length, G, per_group, P_SIZE)
        return (values, delta_one, write_one, read_one, grads)

    def ends_of(number):
        values, delta_one, write_one, read_one, grads = unpack(number)
        local_state, decay_all = segment_end(values, delta_one, rate_grid, write_one)
        return (local_state, decay_all, start_grad(grads, delta_one, rate_grid, read_one))
    slots = jnp.arange(segments, dtype=jnp.int32)
    local_states, decay_all, start_parts = lax.map(ends_of, slots)
    is_root = (parents < 0)[:, None, None, None, None]
    safe_parent = jnp.maximum(parents, 0)
    starts = jnp.zeros_like(local_states)
    for repeat in range(DEPTH - 1):
        end_states = round_half(decay_all[..., None, None] * starts + local_states)
        at_level = (levels == repeat + 1)[:, None, None, None, None]
        starts = jnp.where(at_level, end_states[safe_parent], starts)
    grad_ends = jnp.zeros_like(local_states)
    for repeat in range(DEPTH - 1):
        grad_starts = decay_all[..., None, None] * grad_ends + start_parts
        grad_starts = jnp.where(is_root, 0.0, grad_starts)
        grad_ends = jax.ops.segment_sum(grad_starts, safe_parent, num_segments=segments)

    def backward(number):
        values, delta_one, write_one, read_one, grads = unpack(number)

        def core_map(values, delta_one, write_one, read_one):
            return ssd_forward(values, delta_one, rate_grid, write_one, read_one, starts[number], BLOCK)
        (core_out, end_state), pullback = jax.vjp(core_map, values, delta_one, write_one, read_one)
        grad_values, grad_delta, grad_write, grad_read = pullback((grads, grad_ends[number]))
        result = core_out + skip_grid[None, :, :, None] * values
        grad_values = grad_values + skip_grid[None, :, :, None] * grads
        return (result.reshape(length, H * P_SIZE).astype(jnp.bfloat16), grad_values.reshape(length, H * P_SIZE).astype(jnp.bfloat16), grad_delta.reshape(H, length), grad_write.reshape(length, G * N).astype(jnp.bfloat16), grad_read.reshape(length, G * N).astype(jnp.bfloat16))
    outputs, grad_inputs, grad_deltas, grad_writer, grad_reader = lax.map(backward, slots)
    return (outputs, grad_inputs, grad_deltas, grad_writer, grad_reader)
```

```python
import functools

import jax
import jax.numpy as jnp
from jax import lax
from jax.experimental import pallas as pl
from jax.experimental.pallas import tpu as pltpu
from jax.sharding import PartitionSpec as P

P_SIZE = 64
N = 128
HEADS_PER_GROUP = 32
LENGTH = 256
SEGS = 16
KIDS = 4
F32, BF16 = jnp.float32, jnp.bfloat16
MESH = pl.DeviceIdType.MESH


def dot_nn(a, b):
    return lax.dot_general(a, b, (((1,), (0,)), ((), ())), preferred_element_type=F32)


def dot_nt(a, b):
    return lax.dot_general(a, b, (((1,), (1,)), ((), ())), preferred_element_type=F32)


def dot_tn(a, b):
    return lax.dot_general(a, b, (((0,), (0,)), ((), ())), preferred_element_type=F32)


def halves(v):
    high = v.astype(BF16)
    return high, (v - high.astype(F32)).astype(BF16)


def thirds(v):
    high, rest = v.astype(BF16), v
    rest = v - high.astype(F32)
    mid = rest.astype(BF16)
    return high, mid, (rest - mid.astype(F32)).astype(BF16)


def sum_with(v, ones):
    high, mid, low = thirds(v)
    return dot_nn(high, ones) + (dot_nn(mid, ones) + dot_nn(low, ones))


def kernel(
    heads, owners, wide,
    parents, rates, skips, deltas_hbm, x_hbm, dy_hbm, b_hbm, c_hbm,
    out_hbm, gx_hbm, gd_hbm, gw_hbm, gr_hbm,
    deltas, x, dy, b, c, xh, xl, yh, yl, x2, y2, e1x, e2x, y_in, h_in,
    u_buf, v_buf, a_buf, u_got, v_got, a_got, e_one, s_buf, e_buf, s_all, e_all,
    dc_buf, db_buf, dc_got, db_got, out_v, gx_v, gd_v, gw_v, gr_v, kids, pidx, gidx,
    in_sem, out_sem, su, ru, sv, rv, sa, ra, ss, rs, se, re, sc, rc, sb, rb,
):
    columns = heads * P_SIZE
    rows = LENGTH // owners
    half = N // 2
    seg, head = lax.axis_index("seg"), lax.axis_index("head")
    my_z, my_core = seg // 2, lax.rem(seg, 2)
    group_col = pl.multiple_of((head * heads // HEADS_PER_GROUP) * N, N)

    def load(src, dst, k):
        return pltpu.make_async_copy(src, dst, in_sem.at[k])

    loads = [
        load(deltas_hbm.at[0], deltas, 0),
        load(b_hbm.at[0, :, pl.ds(group_col, N)], b, 1),
        load(x_hbm.at[0], x, 2),
        load(c_hbm.at[0, :, pl.ds(group_col, N)], c, 3),
        load(dy_hbm.at[0], dy, 4),
    ]
    for one in loads:
        one.start()

    barrier = pltpu.get_barrier_semaphore()

    def greet_seg(d, carry):
        pl.semaphore_signal(barrier, inc=1, device_id=(lax.rem(seg + d, SEGS), head), device_id_type=MESH)
        return carry

    def greet_head(d, carry):
        pl.semaphore_signal(barrier, inc=1, device_id=(seg, lax.rem(head + d, owners)), device_id_type=MESH)
        return carry

    lax.fori_loop(1, SEGS, greet_seg, 0)
    lax.fori_loop(1, owners, greet_head, 0)

    def table(s, carry):
        c0 = c1 = c2 = c3 = jnp.int32(SEGS)
        for k in range(SEGS - 1, -1, -1):
            hit = parents[k] == s
            c3 = jnp.where(hit, c2, c3)
            c2 = jnp.where(hit, c1, c2)
            c1 = jnp.where(hit, c0, c1)
            c0 = jnp.where(hit, k, c0)
        kids[KIDS * s] = c0
        kids[KIDS * s + 1] = c1
        kids[KIDS * s + 2] = c2
        kids[KIDS * s + 3] = c3
        p = parents[s]
        g = parents[jnp.maximum(p, 0)]
        pidx[s] = jnp.where(p < 0, SEGS, p)
        gidx[s] = jnp.where(p < 0, SEGS, jnp.where(g < 0, SEGS, g))
        return carry

    u_got[SEGS] = jnp.zeros((half, N), BF16)
    v_got[SEGS] = jnp.zeros((half, N), BF16)
    a_got[SEGS] = jnp.zeros((1, N), F32)
    e_one[SEGS] = jnp.zeros((half, N), F32)

    row_h = lax.broadcasted_iota(jnp.int32, (heads, 1), 0)
    rate_col = jnp.zeros((heads, 1), F32)
    for h in range(heads):
        rate_col = jnp.where(row_h == h, rates[h], rate_col)

    t_row = lax.broadcasted_iota(jnp.int32, (LENGTH, LENGTH), 0)
    t_col = lax.broadcasted_iota(jnp.int32, (LENGTH, LENGTH), 1)
    upto = (t_row <= t_col).astype(BF16)
    causal = t_row >= t_col

    pick_row = lax.rem(lax.broadcasted_iota(jnp.int32, (2 * heads, columns), 0), heads)
    pick_col = lax.broadcasted_iota(jnp.int32, (2 * heads, columns), 1) // P_SIZE
    pick2 = (pick_row == pick_col).astype(BF16)
    pick1 = pick2[:heads]

    loads[0].wait()
    delta = deltas[...]
    run = sum_with(-rate_col * delta, upto)
    mid = run[:, LENGTH - 1 :] * 0.5
    e1 = jnp.exp(run - mid)
    e2 = jnp.exp(mid - run) * delta
    emid = jnp.broadcast_to(jnp.exp(mid), (heads, 8))
    e1s = jnp.concatenate(halves(e1), axis=0)
    e2s = jnp.concatenate(halves(e2), axis=0)
    ems = jnp.concatenate(halves(emid), axis=0)
    em_row = dot_tn(ems, pick2)[:1]

    blocks = [slice(k, k + wide) for k in range(0, columns, wide)]

    loads[1].wait()
    loads[2].wait()
    bt = b[...].T
    for cut in blocks:
        ex = dot_tn(e2s, pick2[:, cut])
        e2x[:, cut] = ex
        scaled = ex * x[:, cut].astype(F32)
        high, low = halves(scaled)
        xh[:, cut] = high
        xl[:, cut] = low
        u_buf[:, cut] = (em_row[:, cut] * (dot_nn(bt, high) + dot_nn(bt, low))).astype(BF16)
    for z in range(SEGS // 2):
        part = em_row[:, z * N : (z + 1) * N]
        a_buf[z] = part * part

    pl.semaphore_wait(barrier, SEGS - 1 + owners - 1)

    def seg_peer(d):
        peer = lax.rem(seg + d, SEGS)
        came = lax.rem(seg - d + SEGS, SEGS)
        return peer, came

    def spot(ref, s):
        z, core = s // 2, lax.rem(s, 2)
        return ref.at[pl.ds(pl.multiple_of(core * half, half), half), pl.ds(pl.multiple_of(z * N, N), N)]

    def up_copy(buf, got, send, recv, d, dst):
        peer, _ = seg_peer(d)
        return pltpu.make_async_remote_copy(
            src_ref=spot(buf, peer), dst_ref=got.at[dst], send_sem=send.at[d], recv_sem=recv.at[d],
            device_id=(peer, head), device_id_type=MESH,
        )

    def a_copy(d, dst):
        peer, _ = seg_peer(d)
        return pltpu.make_async_remote_copy(
            src_ref=a_buf.at[peer // 2], dst_ref=a_got.at[dst], send_sem=sa.at[d], recv_sem=ra.at[d],
            device_id=(peer, head), device_id_type=MESH,
        )

    def down_copy(buf, whole, send, recv, d, owner):
        peer, _ = seg_peer(d)
        return pltpu.make_async_remote_copy(
            src_ref=buf.at[peer], dst_ref=spot(whole, owner), send_sem=send.at[d], recv_sem=recv.at[d],
            device_id=(peer, head), device_id_type=MESH,
        )

    def send_u(d, carry):
        up_copy(u_buf, u_got, su, ru, d, seg).start()
        a_copy(d, seg).start()
        return carry

    lax.fori_loop(1, SEGS, send_u, 0)
    u_got[seg] = spot(u_buf, seg)[...]
    a_got[seg] = a_buf[my_z]

    loads[3].wait()
    loads[4].wait()
    ct = c[...].T
    for cut in blocks:
        ex = dot_tn(e1s, pick2[:, cut])
        e1x[:, cut] = ex
        scaled = ex * dy[:, cut].astype(F32)
        high, low = halves(scaled)
        yh[:, cut] = high
        yl[:, cut] = low
        v_buf[:, cut] = (em_row[:, cut] * (dot_nn(ct, high) + dot_nn(ct, low))).astype(BF16)

    def send_v(d, carry):
        up_copy(v_buf, v_got, sv, rv, d, seg).start()
        return carry

    lax.fori_loop(1, SEGS, send_v, 0)
    v_got[seg] = spot(v_buf, seg)[...]

    lax.fori_loop(0, SEGS, table, 0)
    gram = jnp.where(causal, dot_nt(c[...], b[...]), 0.0)
    gram_t = jnp.where(t_row <= t_col, dot_nt(b[...], c[...]), 0.0)
    gh, gl = halves(gram)
    th, tl = halves(gram_t)
    k_sum = jnp.zeros((LENGTH, LENGTH), F32)
    for cut in blocks:
        x_high, x_low, y_high, y_low = xh[:, cut], xl[:, cut], yh[:, cut], yl[:, cut]
        y_in[:, cut] = e1x[:, cut] * (dot_nn(gh, x_high) + (dot_nn(gh, x_low) + dot_nn(gl, x_high)))
        h_in[:, cut] = e2x[:, cut] * (dot_nn(th, y_high) + (dot_nn(th, y_low) + dot_nn(tl, y_high)))
        k_sum += dot_nt(y_high, x_high) + (dot_nt(y_high, x_low) + dot_nt(y_low, x_high))
        e1x[:, cut] = e1x[:, cut] * em_row[:, cut]
        e2x[:, cut] = e2x[:, cut] * em_row[:, cut]
        x2[:, cut] = (e2x[:, cut] * x[:, cut].astype(F32)).astype(BF16)
        y2[:, cut] = (e1x[:, cut] * dy[:, cut].astype(F32)).astype(BF16)
    k_sum = jnp.where(causal, k_sum, 0.0)
    kh, kl = halves(k_sum)
    dc_buf[...] = dot_nn(kh, b[...]) + dot_nn(kl, b[...])
    db_buf[...] = dot_tn(kh, c[...]) + dot_tn(kl, c[...])

    def wait_u(d, carry):
        _, came = seg_peer(d)
        up_copy(u_buf, u_got, su, ru, d, came).wait_recv()
        a_copy(d, came).wait_recv()
        return carry

    lax.fori_loop(1, SEGS, wait_u, 0)

    def start_of(s):
        p, g = pidx[s], gidx[s]
        s_buf[s] = (a_got[p] * u_got[g].astype(F32) + u_got[p].astype(F32)).astype(BF16)

    def send_s(d, carry):
        peer, _ = seg_peer(d)
        start_of(peer)
        down_copy(s_buf, s_all, ss, rs, d, seg).start()
        return carry

    lax.fori_loop(1, SEGS, send_s, 0)
    start_of(seg)
    spot(s_all, seg)[...] = s_buf[seg]

    def wait_v(d, carry):
        _, came = seg_peer(d)
        up_copy(v_buf, v_got, sv, rv, d, came).wait_recv()
        return carry

    lax.fori_loop(1, SEGS, wait_v, 0)

    def first_e(s, carry):
        total = v_got[kids[KIDS * s]].astype(F32)
        for k in range(1, KIDS):
            total += v_got[kids[KIDS * s + k]].astype(F32)
        e_one[s] = total
        return carry

    lax.fori_loop(0, SEGS, first_e, 0)

    def end_grad(s):
        total = e_one[s]
        for k in range(KIDS):
            kid = kids[KIDS * s + k]
            total += a_got[kid] * e_one[kid]
        e_buf[s] = total.astype(BF16)

    def send_e(d, carry):
        peer, _ = seg_peer(d)
        end_grad(peer)
        down_copy(e_buf, e_all, se, re, d, seg).start()
        return carry

    lax.fori_loop(1, SEGS, send_e, 0)
    end_grad(seg)
    spot(e_all, seg)[...] = e_buf[seg]

    def head_copy(buf, got, send, recv, d, dst):
        peer = lax.rem(head + d, owners)
        return pltpu.make_async_remote_copy(
            src_ref=buf.at[pl.ds(pl.multiple_of(peer * rows, rows), rows)], dst_ref=got.at[dst],
            send_sem=send.at[d], recv_sem=recv.at[d], device_id=(seg, peer), device_id_type=MESH,
        )

    def skip_row(at):
        lane = lax.broadcasted_iota(jnp.int32, (1, wide), 1) // P_SIZE
        row = jnp.zeros((1, wide), F32)
        for h in range(wide // P_SIZE):
            row = jnp.where(lane == h, skips[at // P_SIZE + h], row)
        return row

    def wait_s(d, carry):
        _, came = seg_peer(d)
        down_copy(s_buf, s_all, ss, rs, d, came).wait_recv()
        return carry

    lax.fori_loop(1, SEGS, wait_s, 0)
    d_one = jnp.zeros((heads, LENGTH), F32)
    dc = dc_buf[...]
    for cut in blocks:
        core = y_in[:, cut] + e1x[:, cut] * dot_nn(c[...], s_all[:, cut])
        out_v[:, cut] = (core + skip_row(cut.start) * x[:, cut].astype(F32)).astype(BF16)
        high, low = halves(core * dy[:, cut].astype(F32))
        d_one += dot_nt(pick1[:, cut], high) + dot_nt(pick1[:, cut], low)
        dc += dot_nt(y2[:, cut], s_all[:, cut])
    dc_buf[...] = dc
    out_copy = pltpu.make_async_copy(out_v, out_hbm.at[0], out_sem.at[0])
    out_copy.start()

    def send_dc(d, carry):
        head_copy(dc_buf, dc_got, sc, rc, d, head).start()
        return carry

    lax.fori_loop(1, owners, send_dc, 0)
    dc_got[head] = dc_buf[pl.ds(pl.multiple_of(head * rows, rows), rows)]

    def wait_e(d, carry):
        _, came = seg_peer(d)
        down_copy(e_buf, e_all, se, re, d, came).wait_recv()
        return carry

    lax.fori_loop(1, SEGS, wait_e, 0)
    d_two = jnp.zeros((heads, LENGTH), F32)
    d_last = jnp.zeros((heads, 8), F32)
    db = db_buf[...]
    for cut in blocks:
        ends = e_all[:, cut]
        x_cut = x[:, cut].astype(F32)
        late = e2x[:, cut] * dot_nn(b[...], ends)
        grad = h_in[:, cut] + late
        gx_v[:, cut] = (grad + skip_row(cut.start) * dy[:, cut].astype(F32)).astype(BF16)
        high, low = halves(grad * x_cut)
        d_two += dot_nt(pick1[:, cut], high) + dot_nt(pick1[:, cut], low)
        em = em_row[:, cut]
        both = jnp.sum(ends.astype(F32) * s_all[:, cut].astype(F32), axis=0, keepdims=True)
        tail = jnp.sum(late * x_cut, axis=0, keepdims=True) + em * em * both
        high, low = halves(jnp.broadcast_to(tail, (8, wide)))
        d_last += dot_nt(pick1[:, cut], high) + dot_nt(pick1[:, cut], low)
        db += dot_nt(x2[:, cut], ends)
    db_buf[...] = db

    def send_db(d, carry):
        head_copy(db_buf, db_got, sb, rb, d, head).start()
        return carry

    lax.fori_loop(1, owners, send_db, 0)
    db_got[head] = db_buf[pl.ds(pl.multiple_of(head * rows, rows), rows)]
    gx_copy = pltpu.make_async_copy(gx_v, gx_hbm.at[0], out_sem.at[1])
    gx_copy.start()

    since = (t_row >= t_col).astype(BF16)
    later = sum_with(d_one - d_two, since) + d_last[:, :1]
    gd_v[...] = d_two / delta - rate_col * later
    gd_copy = pltpu.make_async_copy(gd_v, gd_hbm.at[0], out_sem.at[2])
    gd_copy.start()

    share = max(1, HEADS_PER_GROUP // heads)

    def finish(got, buf, send, recv, dst):
        def wait_one(d, carry):
            head_copy(buf, got, send, recv, d, lax.rem(head - d + owners, owners)).wait_recv()
            return carry

        lax.fori_loop(1, owners, wait_one, 0)
        for g in range(owners // share):
            total = got[g * share]
            for k in range(1, share):
                total += got[g * share + k]
            dst[:, g * N : (g + 1) * N] = total.astype(BF16)

    finish(dc_got, dc_buf, sc, rc, gr_v)
    gr_copy = pltpu.make_async_copy(gr_v, gr_hbm.at[0], out_sem.at[3])
    gr_copy.start()
    finish(db_got, db_buf, sb, rb, gw_v)
    gw_copy = pltpu.make_async_copy(gw_v, gw_hbm.at[0], out_sem.at[4])
    gw_copy.start()

    def drain_seg(d, carry):
        up_copy(u_buf, u_got, su, ru, d, seg).wait_send()
        a_copy(d, seg).wait_send()
        up_copy(v_buf, v_got, sv, rv, d, seg).wait_send()
        down_copy(s_buf, s_all, ss, rs, d, seg).wait_send()
        down_copy(e_buf, e_all, se, re, d, seg).wait_send()
        return carry

    def drain_head(d, carry):
        head_copy(dc_buf, dc_got, sc, rc, d, head).wait_send()
        head_copy(db_buf, db_got, sb, rb, d, head).wait_send()
        return carry

    lax.fori_loop(1, SEGS, drain_seg, 0)
    lax.fori_loop(1, owners, drain_head, 0)
    for one in (out_copy, gx_copy, gd_copy, gr_copy, gw_copy):
        one.wait()


def shards(owners, inputs, deltas, rates, skips, writer, reader, grad_out, parents, levels):
    heads = deltas.shape[1]
    columns = inputs.shape[2]
    rows = LENGTH // owners
    half = N // 2
    vm = pltpu.VMEM
    wide_b = lambda: vm((LENGTH, columns), BF16)
    wide_f = lambda: vm((LENGTH, columns), F32)
    sem = lambda n: pltpu.SemaphoreType.DMA((n,))
    anywhere = pl.BlockSpec(memory_space=pl.ANY)
    scalars = pl.BlockSpec(memory_space=pltpu.SMEM)
    return tuple(
        pl.pallas_call(
            functools.partial(kernel, heads, owners, 256),
            out_shape=(
                jax.ShapeDtypeStruct(inputs.shape, BF16),
                jax.ShapeDtypeStruct(inputs.shape, BF16),
                jax.ShapeDtypeStruct(deltas.shape, F32),
                jax.ShapeDtypeStruct((1, rows, writer.shape[2]), BF16),
                jax.ShapeDtypeStruct((1, rows, writer.shape[2]), BF16),
            ),
            in_specs=[scalars] * 3 + [anywhere] * 5,
            out_specs=[anywhere] * 5,
            scratch_shapes=[
                vm((heads, LENGTH), F32), wide_b(), wide_b(), vm((LENGTH, N), BF16), vm((LENGTH, N), BF16),
                wide_b(), wide_b(), wide_b(), wide_b(), wide_b(), wide_b(), wide_f(), wide_f(), wide_f(), wide_f(),
                vm((N, columns), BF16), vm((N, columns), BF16), vm((SEGS // 2, 1, N), F32),
                vm((SEGS + 1, half, N), BF16), vm((SEGS + 1, half, N), BF16), vm((SEGS + 1, 1, N), F32),
                vm((SEGS + 1, half, N), F32), vm((SEGS, half, N), BF16), vm((SEGS, half, N), BF16),
                vm((N, columns), BF16), vm((N, columns), BF16),
                vm((LENGTH, N), F32), vm((LENGTH, N), F32), vm((owners, rows, N), F32), vm((owners, rows, N), F32),
                wide_b(), wide_b(), vm((heads, LENGTH), F32),
                vm((rows, writer.shape[2]), BF16), vm((rows, writer.shape[2]), BF16),
                pltpu.SMEM((KIDS * SEGS,), jnp.int32), pltpu.SMEM((SEGS,), jnp.int32), pltpu.SMEM((SEGS,), jnp.int32),
                sem(5), sem(5),
            ] + [sem(SEGS)] * 10 + [sem(owners)] * 4,
            compiler_params=pltpu.CompilerParams(
                collective_id=0, has_side_effects=True, vmem_limit_bytes=48 * 1024 * 1024
            ),
            name="tree_scan",
        )(parents, rates, skips, deltas, inputs, grad_out, writer, reader)
    )


def solution(mesh):
    placed = (
        P("seg", None, "head"),
        P("seg", "head", None),
        P("head"),
        P("head"),
        P("seg", None, None),
        P("seg", None, None),
        P("seg", None, "head"),
        P(),
        P(),
    )
    return jax.shard_map(
        functools.partial(shards, mesh.shape["head"]),
        mesh=mesh,
        in_specs=placed,
        out_specs=(
            P("seg", None, "head"),
            P("seg", None, "head"),
            P("seg", "head", None),
            P("seg", "head", None),
            P("seg", "head", None),
        ),
        check_vma=False,
    )
```

```python
import functools

import jax
import jax.numpy as jnp
from jax import lax
from jax.experimental import pallas as pl
from jax.experimental.pallas import tpu as pltpu
from jax.sharding import PartitionSpec as P

P_SIZE = 64
N = 128
HEADS_PER_GROUP = 32
LENGTH = 256
SEGS = 16
KIDS = 4
F32, BF16 = jnp.float32, jnp.bfloat16
MESH = pl.DeviceIdType.MESH


def dot_nn(a, b):
    return lax.dot_general(a, b, (((1,), (0,)), ((), ())), preferred_element_type=F32)


def dot_nt(a, b):
    return lax.dot_general(a, b, (((1,), (1,)), ((), ())), preferred_element_type=F32)


def dot_tn(a, b):
    return lax.dot_general(a, b, (((0,), (0,)), ((), ())), preferred_element_type=F32)


def halves(v):
    high = v.astype(BF16)
    return high, (v - high.astype(F32)).astype(BF16)


def thirds(v):
    high, rest = v.astype(BF16), v
    rest = v - high.astype(F32)
    mid = rest.astype(BF16)
    return high, mid, (rest - mid.astype(F32)).astype(BF16)


def nearest(i, n):
    step = (i + 1) // 2
    return jnp.where(lax.rem(i, 2) == 1, step, n - step)


def sum_with(v, ones):
    high, mid, low = thirds(v)
    return dot_nn(high, ones) + (dot_nn(mid, ones) + dot_nn(low, ones))


def kernel(
    heads, owners, wide,
    parents_hbm, rates_hbm, skips_hbm, deltas_hbm, x_hbm, dy_hbm, b_hbm, c_hbm,
    out_v, gx_v, gd_v, gw_v, gr_v,
    deltas, x, dy, b, c, xh, xl, yh, yl, x2, y2, e1x, e2x, y_in, h_in,
    u_buf, v_buf, a_buf, u_got, v_got, a_got, e_one, s_buf, e_buf, s_all, e_all,
    em_buf, dc_buf, db_buf, dc_got, db_got, parents, rates, skips, kids, pidx, gidx,
    in_sem, su, ru, sv, rv, sa, ra, ss, rs, se, re, sc, rc, sb, rb,
):
    columns = heads * P_SIZE
    rows = LENGTH // owners
    half = N // 2
    seg, head = lax.axis_index("seg"), lax.axis_index("head")
    my_z, my_core = seg // 2, lax.rem(seg, 2)
    group_col = pl.multiple_of((head * heads // HEADS_PER_GROUP) * N, N)

    def load(src, dst, k):
        return pltpu.make_async_copy(src, dst, in_sem.at[k])

    loads = [
        load(deltas_hbm.at[0], deltas, 0),
        load(b_hbm.at[0, :, pl.ds(group_col, N)], b, 1),
        load(x_hbm.at[0], x, 2),
        load(c_hbm.at[0, :, pl.ds(group_col, N)], c, 3),
        load(dy_hbm.at[0], dy, 4),
        load(rates_hbm, rates, 5),
        load(parents_hbm, parents, 6),
        load(skips_hbm, skips, 7),
    ]
    for one in loads:
        one.start()

    barrier = pltpu.get_barrier_semaphore()

    def greet_seg(d, carry):
        pl.semaphore_signal(barrier, inc=1, device_id=(lax.rem(seg + d, SEGS), head), device_id_type=MESH)
        return carry

    def greet_head(d, carry):
        pl.semaphore_signal(barrier, inc=1, device_id=(seg, lax.rem(head + d, owners)), device_id_type=MESH)
        return carry

    lax.fori_loop(1, SEGS, greet_seg, 0)
    lax.fori_loop(1, owners, greet_head, 0)

    def table(s, carry):
        c0 = c1 = c2 = c3 = jnp.int32(SEGS)
        for k in range(SEGS - 1, -1, -1):
            hit = parents[k] == s
            c3 = jnp.where(hit, c2, c3)
            c2 = jnp.where(hit, c1, c2)
            c1 = jnp.where(hit, c0, c1)
            c0 = jnp.where(hit, k, c0)
        kids[KIDS * s] = c0
        kids[KIDS * s + 1] = c1
        kids[KIDS * s + 2] = c2
        kids[KIDS * s + 3] = c3
        p = parents[s]
        g = parents[jnp.maximum(p, 0)]
        pidx[s] = jnp.where(p < 0, SEGS, p)
        gidx[s] = jnp.where(p < 0, SEGS, jnp.where(g < 0, SEGS, g))
        return carry

    u_got[SEGS] = jnp.zeros((half, N), BF16)
    v_got[SEGS] = jnp.zeros((half, N), BF16)
    a_got[SEGS] = jnp.zeros((1, N), F32)
    e_one[SEGS] = jnp.zeros((half, N), F32)

    loads[5].wait()
    row_h = lax.broadcasted_iota(jnp.int32, (heads, 1), 0)
    rate_col = jnp.zeros((heads, 1), F32)
    for h in range(heads):
        rate_col = jnp.where(row_h == h, rates[h], rate_col)

    t_row = lax.broadcasted_iota(jnp.int32, (LENGTH, LENGTH), 0)
    t_col = lax.broadcasted_iota(jnp.int32, (LENGTH, LENGTH), 1)
    upto = (t_row <= t_col).astype(BF16)
    causal = t_row >= t_col

    pick_row = lax.rem(lax.broadcasted_iota(jnp.int32, (2 * heads, columns), 0), heads)
    pick_col = lax.broadcasted_iota(jnp.int32, (2 * heads, columns), 1) // P_SIZE
    pick2 = (pick_row == pick_col).astype(BF16)
    pick1 = pick2[:heads]

    loads[0].wait()
    delta = deltas[...]
    run = sum_with(-rate_col * delta, upto)
    mid = run[:, LENGTH - 1 :] * 0.5
    e1 = jnp.exp(run - mid)
    e2 = jnp.exp(mid - run) * delta
    emid = jnp.broadcast_to(jnp.exp(mid), (heads, 8))
    e1s = jnp.concatenate(halves(e1), axis=0)
    e2s = jnp.concatenate(halves(e2), axis=0)
    ems = jnp.concatenate(halves(emid), axis=0)
    em_row = dot_tn(ems, pick2)[:1]

    blocks = [slice(k, k + wide) for k in range(0, columns, wide)]

    loads[1].wait()
    loads[2].wait()
    bt = b[...].T
    for cut in blocks:
        ex = dot_tn(e2s, pick2[:, cut])
        e2x[:, cut] = ex
        scaled = ex * x[:, cut].astype(F32)
        high, low = halves(scaled)
        xh[:, cut] = high
        xl[:, cut] = low
        u_buf[:, cut] = (em_row[:, cut] * (dot_nn(bt, high) + dot_nn(bt, low))).astype(BF16)
    for z in range(SEGS // 2):
        part = em_row[:, z * N : (z + 1) * N]
        em_buf[z] = part
        a_buf[z] = part * part

    pl.semaphore_wait(barrier, SEGS - 1 + owners - 1)

    def seg_peer(i):
        d = nearest(i, SEGS)
        peer = lax.rem(seg + d, SEGS)
        came = lax.rem(seg - d + SEGS, SEGS)
        return peer, came, d

    def spot(ref, s):
        z, core = s // 2, lax.rem(s, 2)
        return ref.at[pl.ds(pl.multiple_of(core * half, half), half), pl.ds(pl.multiple_of(z * N, N), N)]

    def up_copy(buf, got, send, recv, i, dst):
        peer, _, d = seg_peer(i)
        return pltpu.make_async_remote_copy(
            src_ref=spot(buf, peer), dst_ref=got.at[dst], send_sem=send.at[d], recv_sem=recv.at[d],
            device_id=(peer, head), device_id_type=MESH,
        )

    def a_copy(i, dst):
        peer, _, d = seg_peer(i)
        return pltpu.make_async_remote_copy(
            src_ref=a_buf.at[peer // 2], dst_ref=a_got.at[dst], send_sem=sa.at[d], recv_sem=ra.at[d],
            device_id=(peer, head), device_id_type=MESH,
        )

    def down_copy(buf, whole, send, recv, i, owner):
        peer, _, d = seg_peer(i)
        return pltpu.make_async_remote_copy(
            src_ref=buf.at[peer], dst_ref=spot(whole, owner), send_sem=send.at[d], recv_sem=recv.at[d],
            device_id=(peer, head), device_id_type=MESH,
        )

    def send_u(d, carry):
        up_copy(u_buf, u_got, su, ru, d, seg).start()
        a_copy(d, seg).start()
        return carry

    lax.fori_loop(1, SEGS, send_u, 0)
    u_got[seg] = spot(u_buf, seg)[...]
    a_got[seg] = a_buf[my_z]

    loads[3].wait()
    loads[4].wait()
    ct = c[...].T
    for cut in blocks:
        ex = dot_tn(e1s, pick2[:, cut])
        e1x[:, cut] = ex
        scaled = ex * dy[:, cut].astype(F32)
        high, low = halves(scaled)
        yh[:, cut] = high
        yl[:, cut] = low
        v_buf[:, cut] = (em_row[:, cut] * (dot_nn(ct, high) + dot_nn(ct, low))).astype(BF16)

    loads[6].wait()
    loads[7].wait()
    lax.fori_loop(0, SEGS, table, 0)
    gram = jnp.where(causal, dot_nt(c[...], b[...]), 0.0)
    gram_t = jnp.where(t_row <= t_col, dot_nt(b[...], c[...]), 0.0)
    gh, gl = halves(gram)
    th, tl = halves(gram_t)
    k_sum = jnp.zeros((LENGTH, LENGTH), F32)
    for cut in blocks:
        x_high, x_low, y_high, y_low = xh[:, cut], xl[:, cut], yh[:, cut], yl[:, cut]
        y_in[:, cut] = e1x[:, cut] * (dot_nn(gh, x_high) + (dot_nn(gh, x_low) + dot_nn(gl, x_high)))
        h_in[:, cut] = e2x[:, cut] * (dot_nn(th, y_high) + (dot_nn(th, y_low) + dot_nn(tl, y_high)))
        k_sum += dot_nt(y_high, x_high) + (dot_nt(y_high, x_low) + dot_nt(y_low, x_high))
        e1x[:, cut] = e1x[:, cut] * em_row[:, cut]
        e2x[:, cut] = e2x[:, cut] * em_row[:, cut]
        x2[:, cut] = (e2x[:, cut] * x[:, cut].astype(F32)).astype(BF16)
        y2[:, cut] = (e1x[:, cut] * dy[:, cut].astype(F32)).astype(BF16)
    k_sum = jnp.where(causal, k_sum, 0.0)
    kh, kl = halves(k_sum)
    dc_buf[...] = dot_nn(kh, b[...]) + dot_nn(kl, b[...])
    db_buf[...] = dot_tn(kh, c[...]) + dot_tn(kl, c[...])

    def send_v(d, carry):
        up_copy(v_buf, v_got, sv, rv, d, seg).start()
        return carry

    lax.fori_loop(1, SEGS, send_v, 0)
    v_got[seg] = spot(v_buf, seg)[...]

    def wait_u(d, carry):
        _, came, _ = seg_peer(d)
        up_copy(u_buf, u_got, su, ru, d, came).wait_recv()
        a_copy(d, came).wait_recv()
        return carry

    lax.fori_loop(1, SEGS, wait_u, 0)

    def start_of(s):
        p, g = pidx[s], gidx[s]
        s_buf[s] = (a_got[p] * u_got[g].astype(F32) + u_got[p].astype(F32)).astype(BF16)

    def send_s(d, carry):
        peer, _, _ = seg_peer(d)
        start_of(peer)
        down_copy(s_buf, s_all, ss, rs, d, seg).start()
        return carry

    lax.fori_loop(1, SEGS, send_s, 0)
    start_of(seg)
    spot(s_all, seg)[...] = s_buf[seg]

    def wait_v(d, carry):
        _, came, _ = seg_peer(d)
        up_copy(v_buf, v_got, sv, rv, d, came).wait_recv()
        return carry

    lax.fori_loop(1, SEGS, wait_v, 0)

    def first_e(s, carry):
        total = v_got[kids[KIDS * s]].astype(F32)
        for k in range(1, KIDS):
            total += v_got[kids[KIDS * s + k]].astype(F32)
        e_one[s] = total
        return carry

    lax.fori_loop(0, SEGS, first_e, 0)

    def end_grad(s):
        total = e_one[s]
        for k in range(KIDS):
            kid = kids[KIDS * s + k]
            total += a_got[kid] * e_one[kid]
        e_buf[s] = total.astype(BF16)

    def send_e(d, carry):
        peer, _, _ = seg_peer(d)
        end_grad(peer)
        down_copy(e_buf, e_all, se, re, d, seg).start()
        return carry

    lax.fori_loop(1, SEGS, send_e, 0)
    end_grad(seg)
    spot(e_all, seg)[...] = e_buf[seg]

    def head_copy(buf, got, send, recv, d, dst):
        peer = lax.rem(head + d, owners)
        return pltpu.make_async_remote_copy(
            src_ref=buf.at[pl.ds(pl.multiple_of(peer * rows, rows), rows)], dst_ref=got.at[dst],
            send_sem=send.at[d], recv_sem=recv.at[d], device_id=(seg, peer), device_id_type=MESH,
        )

    lane = lax.broadcasted_iota(jnp.int32, (1, N), 1)
    near_rows = lax.broadcasted_iota(jnp.int32, (heads, N), 0)
    near_lane = lax.broadcasted_iota(jnp.int32, (heads, N), 1) // P_SIZE

    def zone(i):
        z = lax.rem(my_z + nearest(i, SEGS // 2), SEGS // 2)
        at = pl.ds(pl.multiple_of(z * N, N), N)
        skip = jnp.where(lane < P_SIZE, skips[2 * z], skips[2 * z + 1])
        pick = (near_rows == near_lane + 2 * z).astype(BF16)
        return z, at, skip, pick

    def wait_zone(buf, whole, send, recv, i):
        first = 1 if i == 0 else 0
        for core in range(first, 2):
            if i == 0:
                d = jnp.where(my_core == 0, 1, SEGS - 1)
            else:
                d = lax.rem(2 * nearest(i, SEGS // 2) + core - my_core + SEGS, SEGS)
            came = lax.rem(seg + d, SEGS)
            there = lax.rem(SEGS - d, SEGS)
            pltpu.make_async_remote_copy(
                src_ref=buf.at[came], dst_ref=spot(whole, came), send_sem=send.at[d], recv_sem=recv.at[there],
                device_id=(came, head), device_id_type=MESH,
            ).wait_recv()

    d_one = jnp.zeros((heads, LENGTH), F32)
    dc = dc_buf[...]
    for i in range(SEGS // 2):
        wait_zone(s_buf, s_all, ss, rs, i)
        z, at, skip, pick = zone(i)
        starts = s_all[:, at]
        core = y_in[:, at] + e1x[:, at] * dot_nn(c[...], starts)
        out_v[0, :, at] = (core + skip * x[:, at].astype(F32)).astype(BF16)
        high, low = halves(core * dy[:, at].astype(F32))
        d_one += dot_nt(pick, high) + dot_nt(pick, low)
        dc += dot_nt(y2[:, at], starts)
    dc_buf[...] = dc

    def send_dc(d, carry):
        head_copy(dc_buf, dc_got, sc, rc, d, head).start()
        return carry

    lax.fori_loop(1, owners, send_dc, 0)
    dc_got[head] = dc_buf[pl.ds(pl.multiple_of(head * rows, rows), rows)]

    d_two = jnp.zeros((heads, LENGTH), F32)
    d_last = jnp.zeros((heads, 8), F32)
    db = db_buf[...]
    for i in range(SEGS // 2):
        wait_zone(e_buf, e_all, se, re, i)
        z, at, skip, pick = zone(i)
        ends = e_all[:, at]
        x_cut = x[:, at].astype(F32)
        late = e2x[:, at] * dot_nn(b[...], ends)
        grad = h_in[:, at] + late
        gx_v[0, :, at] = (grad + skip * dy[:, at].astype(F32)).astype(BF16)
        high, low = halves(grad * x_cut)
        d_two += dot_nt(pick, high) + dot_nt(pick, low)
        both = jnp.sum(ends.astype(F32) * s_all[:, at].astype(F32), axis=0, keepdims=True)
        tail = jnp.sum(late * x_cut, axis=0, keepdims=True) + a_buf[z] * both
        high, low = halves(jnp.broadcast_to(tail, (8, N)))
        d_last += dot_nt(pick, high) + dot_nt(pick, low)
        db += dot_nt(x2[:, at], ends)
    db_buf[...] = db

    def send_db(d, carry):
        head_copy(db_buf, db_got, sb, rb, d, head).start()
        return carry

    lax.fori_loop(1, owners, send_db, 0)
    db_got[head] = db_buf[pl.ds(pl.multiple_of(head * rows, rows), rows)]

    since = (t_row >= t_col).astype(BF16)
    later = sum_with(d_one - d_two, since) + d_last[:, :1]
    gd_v[0] = d_two / delta - rate_col * later

    share = max(1, HEADS_PER_GROUP // heads)

    def finish(got, buf, send, recv, dst):
        def wait_one(d, carry):
            head_copy(buf, got, send, recv, d, lax.rem(head - d + owners, owners)).wait_recv()
            return carry

        lax.fori_loop(1, owners, wait_one, 0)
        for g in range(owners // share):
            total = got[g * share]
            for k in range(1, share):
                total += got[g * share + k]
            dst[0, :, g * N : (g + 1) * N] = total.astype(BF16)

    finish(dc_got, dc_buf, sc, rc, gr_v)
    finish(db_got, db_buf, sb, rb, gw_v)

    def drain_seg(d, carry):
        up_copy(u_buf, u_got, su, ru, d, seg).wait_send()
        a_copy(d, seg).wait_send()
        up_copy(v_buf, v_got, sv, rv, d, seg).wait_send()
        down_copy(s_buf, s_all, ss, rs, d, seg).wait_send()
        down_copy(e_buf, e_all, se, re, d, seg).wait_send()
        return carry

    def drain_head(d, carry):
        head_copy(dc_buf, dc_got, sc, rc, d, head).wait_send()
        head_copy(db_buf, db_got, sb, rb, d, head).wait_send()
        return carry

    lax.fori_loop(1, SEGS, drain_seg, 0)
    lax.fori_loop(1, owners, drain_head, 0)


def store(*refs):
    sems = refs[-1]
    done = len(refs) // 2
    copies = [pltpu.make_async_copy(refs[k], refs[done + k], sems.at[k]) for k in range(done)]
    for one in copies:
        one.start()
    for one in copies:
        one.wait()


def shards(owners, inputs, deltas, rates, skips, writer, reader, grad_out, parents, levels):
    heads = deltas.shape[1]
    columns = inputs.shape[2]
    rows = LENGTH // owners
    half = N // 2
    vm = pltpu.VMEM
    wide_b = lambda: vm((LENGTH, columns), BF16)
    wide_f = lambda: vm((LENGTH, columns), F32)
    sem = lambda n: pltpu.SemaphoreType.DMA((n,))
    anywhere = pl.BlockSpec(memory_space=pltpu.HBM)
    vectors = pl.BlockSpec(memory_space=pltpu.VMEM)
    results = (
        jax.ShapeDtypeStruct(inputs.shape, BF16),
        jax.ShapeDtypeStruct(inputs.shape, BF16),
        jax.ShapeDtypeStruct(deltas.shape, F32),
        jax.ShapeDtypeStruct((1, rows, writer.shape[2]), BF16),
        jax.ShapeDtypeStruct((1, rows, writer.shape[2]), BF16),
    )
    made = pl.pallas_call(
        functools.partial(kernel, heads, owners, 256),
        out_shape=results,
        in_specs=[anywhere] * 8,
        out_specs=[vectors] * 5,
        scratch_shapes=[
            vm((heads, LENGTH), F32), wide_b(), wide_b(), vm((LENGTH, N), BF16), vm((LENGTH, N), BF16),
            wide_b(), wide_b(), wide_b(), wide_b(), wide_b(), wide_b(), wide_f(), wide_f(), wide_f(), wide_f(),
            vm((N, columns), BF16), vm((N, columns), BF16), vm((SEGS // 2, 1, N), F32),
            vm((SEGS + 1, half, N), BF16), vm((SEGS + 1, half, N), BF16), vm((SEGS + 1, 1, N), F32),
            vm((SEGS + 1, half, N), F32), vm((SEGS, half, N), BF16), vm((SEGS, half, N), BF16),
            vm((N, columns), BF16), vm((N, columns), BF16), vm((SEGS // 2, 1, N), F32),
            vm((LENGTH, N), F32), vm((LENGTH, N), F32), vm((owners, rows, N), F32), vm((owners, rows, N), F32),
            pltpu.SMEM((SEGS,), jnp.int32), pltpu.SMEM((heads,), F32), pltpu.SMEM((heads,), F32),
            pltpu.SMEM((KIDS * SEGS,), jnp.int32), pltpu.SMEM((SEGS,), jnp.int32), pltpu.SMEM((SEGS,), jnp.int32),
            sem(8),
        ] + [sem(SEGS)] * 10 + [sem(owners)] * 4,
        compiler_params=pltpu.CompilerParams(
            collective_id=0, has_side_effects=True, vmem_limit_bytes=48 * 1024 * 1024
        ),
        name="tree_scan",
    )(*(pltpu.with_memory_space_constraint(a, pltpu.HBM) for a in (parents, rates, skips, deltas, inputs, grad_out, writer, reader)))
    return tuple(
        pl.pallas_call(
            store,
            out_shape=results,
            in_specs=[vectors] * 5,
            out_specs=[anywhere] * 5,
            scratch_shapes=[sem(5)],
            compiler_params=pltpu.CompilerParams(vmem_limit_bytes=32 * 1024 * 1024),
            name="store",
        )(*made)
    )


def solution(mesh):
    placed = (
        P("seg", None, "head"),
        P("seg", "head", None),
        P("head"),
        P("head"),
        P("seg", None, None),
        P("seg", None, None),
        P("seg", None, "head"),
        P(),
        P(),
    )
    return jax.shard_map(
        functools.partial(shards, mesh.shape["head"]),
        mesh=mesh,
        in_specs=placed,
        out_specs=(
            P("seg", None, "head"),
            P("seg", None, "head"),
            P("seg", "head", None),
            P("seg", "head", None),
            P("seg", "head", None),
        ),
        check_vma=False,
    )
```

```python
import functools

import jax
import jax.numpy as jnp
from jax import lax
from jax.experimental import pallas as pl
from jax.experimental.pallas import tpu as pltpu
from jax.sharding import PartitionSpec as P

P_SIZE = 64
N = 128
HEADS_PER_GROUP = 32
LENGTH = 256
SEGS = 16
KIDS = 4
F32, BF16 = jnp.float32, jnp.bfloat16
MESH = pl.DeviceIdType.MESH


def dot_nn(a, b):
    return lax.dot_general(a, b, (((1,), (0,)), ((), ())), preferred_element_type=F32)


def dot_nt(a, b):
    return lax.dot_general(a, b, (((1,), (1,)), ((), ())), preferred_element_type=F32)


def dot_tn(a, b):
    return lax.dot_general(a, b, (((0,), (0,)), ((), ())), preferred_element_type=F32)


def halves(v):
    high = v.astype(BF16)
    return high, (v - high.astype(F32)).astype(BF16)


def thirds(v):
    high, rest = v.astype(BF16), v
    rest = v - high.astype(F32)
    mid = rest.astype(BF16)
    return high, mid, (rest - mid.astype(F32)).astype(BF16)


def nearest(i, n):
    step = (i + 1) // 2
    return jnp.where(lax.rem(i, 2) == 1, step, n - step)


def sum_with(v, ones):
    high, mid, low = thirds(v)
    return dot_nn(high, ones) + (dot_nn(mid, ones) + dot_nn(low, ones))


def kernel(
    heads, owners, wide,
    parents_hbm, rates_hbm, skips_hbm, deltas_hbm, x_hbm, dy_hbm, b_hbm, c_hbm,
    out_v, gx_v, gd_v, gw_v, gr_v,
    deltas, x, dy, b, c, xh, xl, yh, yl, x2, x2l, y2, e1x, e2x, y_in, h_in,
    u_buf, v_buf, a_buf, u_got, v_got, a_got, e_one, s_buf, e_buf, s_all, e_all,
    em_buf, dc_buf, db_buf, db_low, dc_got, db_got, parents, rates, skips, kids, pidx, gidx,
    in_sem, su, ru, sv, rv, sa, ra, ss, rs, se, re, sc, rc, sb, rb,
):
    columns = heads * P_SIZE
    rows = LENGTH // owners
    half = N // 2
    seg, head = lax.axis_index("seg"), lax.axis_index("head")
    my_z, my_core = seg // 2, lax.rem(seg, 2)
    group_col = pl.multiple_of((head * heads // HEADS_PER_GROUP) * N, N)

    def load(src, dst, k):
        return pltpu.make_async_copy(src, dst, in_sem.at[k])

    loads = [
        load(deltas_hbm.at[0], deltas, 0),
        load(b_hbm.at[0, :, pl.ds(group_col, N)], b, 1),
        load(x_hbm.at[0], x, 2),
        load(c_hbm.at[0, :, pl.ds(group_col, N)], c, 3),
        load(dy_hbm.at[0], dy, 4),
        load(rates_hbm, rates, 5),
        load(parents_hbm, parents, 6),
        load(skips_hbm, skips, 7),
    ]
    for one in loads:
        one.start()

    barrier = pltpu.get_barrier_semaphore()

    def greet_seg(d, carry):
        pl.semaphore_signal(barrier, inc=1, device_id=(lax.rem(seg + d, SEGS), head), device_id_type=MESH)
        return carry

    def greet_head(d, carry):
        pl.semaphore_signal(barrier, inc=1, device_id=(seg, lax.rem(head + d, owners)), device_id_type=MESH)
        return carry

    lax.fori_loop(1, SEGS, greet_seg, 0)
    lax.fori_loop(1, owners, greet_head, 0)

    def table(s, carry):
        c0 = c1 = c2 = c3 = jnp.int32(SEGS)
        for k in range(SEGS - 1, -1, -1):
            hit = parents[k] == s
            c3 = jnp.where(hit, c2, c3)
            c2 = jnp.where(hit, c1, c2)
            c1 = jnp.where(hit, c0, c1)
            c0 = jnp.where(hit, k, c0)
        kids[KIDS * s] = c0
        kids[KIDS * s + 1] = c1
        kids[KIDS * s + 2] = c2
        kids[KIDS * s + 3] = c3
        p = parents[s]
        g = parents[jnp.maximum(p, 0)]
        pidx[s] = jnp.where(p < 0, SEGS, p)
        gidx[s] = jnp.where(p < 0, SEGS, jnp.where(g < 0, SEGS, g))
        return carry

    u_got[SEGS] = jnp.zeros((half, N), BF16)
    v_got[SEGS] = jnp.zeros((half, N), BF16)
    a_got[SEGS] = jnp.zeros((1, N), F32)
    e_one[SEGS] = jnp.zeros((half, N), F32)

    loads[5].wait()
    row_h = lax.broadcasted_iota(jnp.int32, (heads, 1), 0)
    rate_col = jnp.zeros((heads, 1), F32)
    for h in range(heads):
        rate_col = jnp.where(row_h == h, rates[h], rate_col)

    t_row = lax.broadcasted_iota(jnp.int32, (LENGTH, LENGTH), 0)
    t_col = lax.broadcasted_iota(jnp.int32, (LENGTH, LENGTH), 1)
    upto = (t_row <= t_col).astype(BF16)
    causal = t_row >= t_col

    pick_row = lax.rem(lax.broadcasted_iota(jnp.int32, (2 * heads, columns), 0), heads)
    pick_col = lax.broadcasted_iota(jnp.int32, (2 * heads, columns), 1) // P_SIZE
    pick2 = (pick_row == pick_col).astype(BF16)
    pick1 = pick2[:heads]

    loads[0].wait()
    delta = deltas[...]
    run = sum_with(-rate_col * delta, upto)
    mid = run[:, LENGTH - 1 :] * 0.5
    e1 = jnp.exp(run - mid)
    e2 = jnp.exp(mid - run) * delta
    emid = jnp.broadcast_to(jnp.exp(mid), (heads, 8))
    e1s = jnp.concatenate(halves(e1), axis=0)
    e2s = jnp.concatenate(halves(e2), axis=0)
    ems = jnp.concatenate(halves(emid), axis=0)
    em_row = dot_tn(ems, pick2)[:1]

    blocks = [slice(k, k + wide) for k in range(0, columns, wide)]

    for z in range(SEGS // 2):
        part = em_row[:, z * N : (z + 1) * N]
        em_buf[z] = part
        a_buf[z] = part * part

    def seg_peer(i):
        d = nearest(i, SEGS)
        peer = lax.rem(seg + d, SEGS)
        came = lax.rem(seg - d + SEGS, SEGS)
        return peer, came, d

    def spot(ref, s):
        z, core = s // 2, lax.rem(s, 2)
        return ref.at[pl.ds(pl.multiple_of(core * half, half), half), pl.ds(pl.multiple_of(z * N, N), N)]

    def up_copy(buf, got, send, recv, i, dst):
        peer, _, d = seg_peer(i)
        return pltpu.make_async_remote_copy(
            src_ref=spot(buf, peer), dst_ref=got.at[dst], send_sem=send.at[d], recv_sem=recv.at[d],
            device_id=(peer, head), device_id_type=MESH,
        )

    def a_copy(i, dst):
        peer, _, d = seg_peer(i)
        return pltpu.make_async_remote_copy(
            src_ref=a_buf.at[peer // 2], dst_ref=a_got.at[dst], send_sem=sa.at[d], recv_sem=ra.at[d],
            device_id=(peer, head), device_id_type=MESH,
        )

    def down_copy(buf, whole, send, recv, i, owner):
        peer, _, d = seg_peer(i)
        return pltpu.make_async_remote_copy(
            src_ref=buf.at[peer], dst_ref=spot(whole, owner), send_sem=send.at[d], recv_sem=recv.at[d],
            device_id=(peer, head), device_id_type=MESH,
        )

    part_row = lax.rem(lax.broadcasted_iota(jnp.int32, (2 * heads, N), 0), heads)
    part_lane = lax.broadcasted_iota(jnp.int32, (2 * heads, N), 1) // P_SIZE
    loads[1].wait()
    bt = b[...].T
    loads[2].wait()
    for i in range(SEGS // 2):
        ahead = nearest(i, SEGS // 2) if i else 0
        z = lax.rem(my_z + ahead, SEGS // 2)
        at = pl.ds(pl.multiple_of(z * N, N), N)
        ex = dot_tn(e2s, (part_row == part_lane + 2 * z).astype(BF16))
        e2x[:, at] = ex
        scaled = ex * x[:, at].astype(F32)
        high, low = halves(scaled)
        xh[:, at] = high
        xl[:, at] = low
        u_buf[:, at] = (em_buf[z] * (dot_nn(bt, high) + dot_nn(bt, low))).astype(BF16)
        if i == 0:
            pl.semaphore_wait(barrier, SEGS - 1 + owners - 1)
            u_got[seg] = spot(u_buf, seg)[...]
            a_got[seg] = a_buf[my_z]
        for core in range(1 if i == 0 else 0, 2):
            peer = seg + 1 - 2 * my_core if i == 0 else 2 * z + core
            d = lax.rem(peer - seg + SEGS, SEGS)
            pltpu.make_async_remote_copy(
                src_ref=spot(u_buf, peer), dst_ref=u_got.at[seg], send_sem=su.at[d], recv_sem=ru.at[d],
                device_id=(peer, head), device_id_type=MESH,
            ).start()
            pltpu.make_async_remote_copy(
                src_ref=a_buf.at[z], dst_ref=a_got.at[seg], send_sem=sa.at[d], recv_sem=ra.at[d],
                device_id=(peer, head), device_id_type=MESH,
            ).start()

    loads[3].wait()
    loads[4].wait()
    ct = c[...].T
    for cut in blocks:
        ex = dot_tn(e1s, pick2[:, cut])
        e1x[:, cut] = ex
        scaled = ex * dy[:, cut].astype(F32)
        high, low = halves(scaled)
        yh[:, cut] = high
        yl[:, cut] = low
        v_buf[:, cut] = (em_row[:, cut] * (dot_nn(ct, high) + dot_nn(ct, low))).astype(BF16)

    loads[6].wait()
    loads[7].wait()
    lax.fori_loop(0, SEGS, table, 0)
    gram = jnp.where(causal, dot_nt(c[...], b[...]), 0.0)
    gram_t = jnp.where(t_row <= t_col, dot_nt(b[...], c[...]), 0.0)
    gh, gl = halves(gram)
    th, tl = halves(gram_t)
    k_sum = jnp.zeros((LENGTH, LENGTH), F32)
    for cut in blocks:
        x_high, x_low, y_high, y_low = xh[:, cut], xl[:, cut], yh[:, cut], yl[:, cut]
        y_in[:, cut] = e1x[:, cut] * (dot_nn(gh, x_high) + (dot_nn(gh, x_low) + dot_nn(gl, x_high)))
        h_in[:, cut] = e2x[:, cut] * (dot_nn(th, y_high) + (dot_nn(th, y_low) + dot_nn(tl, y_high)))
        k_sum += dot_nt(y_high, x_high) + (dot_nt(y_high, x_low) + dot_nt(y_low, x_high))
        e1x[:, cut] = e1x[:, cut] * em_row[:, cut]
        e2x[:, cut] = e2x[:, cut] * em_row[:, cut]
        high, low = halves(e2x[:, cut] * x[:, cut].astype(F32))
        x2[:, cut] = high
        x2l[:, cut] = low
        y2[:, cut] = (e1x[:, cut] * dy[:, cut].astype(F32)).astype(BF16)
    k_sum = jnp.where(causal, k_sum, 0.0)
    kh, kl = halves(k_sum)
    dc_buf[...] = dot_nn(kh, b[...]) + dot_nn(kl, b[...])
    db_buf[...] = dot_tn(kh, c[...]) + dot_tn(kl, c[...])

    def send_v(d, carry):
        up_copy(v_buf, v_got, sv, rv, d, seg).start()
        return carry

    lax.fori_loop(1, SEGS, send_v, 0)
    v_got[seg] = spot(v_buf, seg)[...]

    def wait_u(d, carry):
        _, came, _ = seg_peer(d)
        up_copy(u_buf, u_got, su, ru, d, came).wait_recv()
        a_copy(d, came).wait_recv()
        return carry

    lax.fori_loop(1, SEGS, wait_u, 0)

    def start_of(s):
        p, g = pidx[s], gidx[s]
        s_buf[s] = (a_got[p] * u_got[g].astype(F32) + u_got[p].astype(F32)).astype(BF16)

    def send_s(d, carry):
        peer, _, _ = seg_peer(d)
        start_of(peer)
        down_copy(s_buf, s_all, ss, rs, d, seg).start()
        return carry

    lax.fori_loop(1, SEGS, send_s, 0)
    start_of(seg)
    spot(s_all, seg)[...] = s_buf[seg]

    def wait_v(d, carry):
        _, came, _ = seg_peer(d)
        up_copy(v_buf, v_got, sv, rv, d, came).wait_recv()
        return carry

    lax.fori_loop(1, SEGS, wait_v, 0)

    def first_e(s, carry):
        total = v_got[kids[KIDS * s]].astype(F32)
        for k in range(1, KIDS):
            total += v_got[kids[KIDS * s + k]].astype(F32)
        e_one[s] = total
        return carry

    lax.fori_loop(0, SEGS, first_e, 0)

    def end_grad(s):
        total = e_one[s]
        for k in range(KIDS):
            kid = kids[KIDS * s + k]
            total += a_got[kid] * e_one[kid]
        e_buf[s] = total.astype(BF16)

    def send_e(d, carry):
        peer, _, _ = seg_peer(d)
        end_grad(peer)
        down_copy(e_buf, e_all, se, re, d, seg).start()
        return carry

    lax.fori_loop(1, SEGS, send_e, 0)
    end_grad(seg)
    spot(e_all, seg)[...] = e_buf[seg]

    def head_copy(buf, got, send, recv, d, dst):
        peer = lax.rem(head + d, owners)
        return pltpu.make_async_remote_copy(
            src_ref=buf.at[pl.ds(pl.multiple_of(peer * rows, rows), rows)], dst_ref=got.at[dst],
            send_sem=send.at[d], recv_sem=recv.at[d], device_id=(seg, peer), device_id_type=MESH,
        )

    lane = lax.broadcasted_iota(jnp.int32, (1, N), 1)
    near_rows = lax.broadcasted_iota(jnp.int32, (heads, N), 0)
    near_lane = lax.broadcasted_iota(jnp.int32, (heads, N), 1) // P_SIZE

    def zone(i):
        z = lax.rem(my_z + nearest(i, SEGS // 2), SEGS // 2)
        at = pl.ds(pl.multiple_of(z * N, N), N)
        skip = jnp.where(lane < P_SIZE, skips[2 * z], skips[2 * z + 1])
        pick = (near_rows == near_lane + 2 * z).astype(BF16)
        return z, at, skip, pick

    def wait_zone(buf, whole, send, recv, i):
        first = 1 if i == 0 else 0
        for core in range(first, 2):
            if i == 0:
                d = jnp.where(my_core == 0, 1, SEGS - 1)
            else:
                d = lax.rem(2 * nearest(i, SEGS // 2) + core - my_core + SEGS, SEGS)
            came = lax.rem(seg + d, SEGS)
            there = lax.rem(SEGS - d, SEGS)
            pltpu.make_async_remote_copy(
                src_ref=buf.at[came], dst_ref=spot(whole, came), send_sem=send.at[d], recv_sem=recv.at[there],
                device_id=(came, head), device_id_type=MESH,
            ).wait_recv()

    d_one = jnp.zeros((heads, LENGTH), F32)
    dc = dc_buf[...]
    for i in range(SEGS // 2):
        wait_zone(s_buf, s_all, ss, rs, i)
        z, at, skip, pick = zone(i)
        starts = s_all[:, at]
        core = y_in[:, at] + e1x[:, at] * dot_nn(c[...], starts)
        out_v[0, :, at] = (core + skip * x[:, at].astype(F32)).astype(BF16)
        high, low = halves(core * dy[:, at].astype(F32))
        d_one += dot_nt(pick, high) + dot_nt(pick, low)
        dc += dot_nt(y2[:, at], starts)
    dc_buf[...] = dc

    def send_dc(d, carry):
        head_copy(dc_buf, dc_got, sc, rc, d, head).start()
        return carry

    lax.fori_loop(1, owners, send_dc, 0)
    dc_got[head] = dc_buf[pl.ds(pl.multiple_of(head * rows, rows), rows)]

    d_two = jnp.zeros((heads, LENGTH), F32)
    d_last = jnp.zeros((heads, 8), F32)
    db = db_buf[...]
    for i in range(SEGS // 2):
        wait_zone(e_buf, e_all, se, re, i)
        z, at, skip, pick = zone(i)
        ends = e_all[:, at]
        x_cut = x[:, at].astype(F32)
        late = e2x[:, at] * dot_nn(b[...], ends)
        grad = h_in[:, at] + late
        gx_v[0, :, at] = (grad + skip * dy[:, at].astype(F32)).astype(BF16)
        high, low = halves(grad * x_cut)
        d_two += dot_nt(pick, high) + dot_nt(pick, low)
        both = jnp.sum(ends.astype(F32) * s_all[:, at].astype(F32), axis=0, keepdims=True)
        tail = jnp.sum(late * x_cut, axis=0, keepdims=True) + a_buf[z] * both
        high, low = halves(jnp.broadcast_to(tail, (8, N)))
        d_last += dot_nt(pick, high) + dot_nt(pick, low)
        db += dot_nt(x2[:, at], ends) + dot_nt(x2l[:, at], ends)
    db_low[...] = db.astype(BF16)

    def send_db(d, carry):
        head_copy(db_low, db_got, sb, rb, d, head).start()
        return carry

    lax.fori_loop(1, owners, send_db, 0)
    db_got[head] = db_low[pl.ds(pl.multiple_of(head * rows, rows), rows)]

    since = (t_row >= t_col).astype(BF16)
    later = sum_with(d_one - d_two, since) + d_last[:, :1]
    gd_v[0] = d_two / delta - rate_col * later

    share = max(1, HEADS_PER_GROUP // heads)

    def finish(got, buf, send, recv, dst):
        def wait_one(d, carry):
            head_copy(buf, got, send, recv, d, lax.rem(head - d + owners, owners)).wait_recv()
            return carry

        lax.fori_loop(1, owners, wait_one, 0)
        for g in range(owners // share):
            total = got[g * share].astype(F32)
            for k in range(1, share):
                total += got[g * share + k].astype(F32)
            dst[0, :, g * N : (g + 1) * N] = total.astype(BF16)

    finish(dc_got, dc_buf, sc, rc, gr_v)
    def drain_dc(d, carry):
        head_copy(dc_buf, dc_got, sc, rc, d, head).wait_send()
        return carry

    def drain_seg(d, carry):
        up_copy(u_buf, u_got, su, ru, d, seg).wait_send()
        a_copy(d, seg).wait_send()
        up_copy(v_buf, v_got, sv, rv, d, seg).wait_send()
        down_copy(s_buf, s_all, ss, rs, d, seg).wait_send()
        down_copy(e_buf, e_all, se, re, d, seg).wait_send()
        return carry

    lax.fori_loop(1, owners, drain_dc, 0)
    lax.fori_loop(1, SEGS, drain_seg, 0)

    finish(db_got, db_low, sb, rb, gw_v)

    def drain_head(d, carry):
        head_copy(db_low, db_got, sb, rb, d, head).wait_send()
        return carry

    lax.fori_loop(1, owners, drain_head, 0)


def store(*refs):
    sems = refs[-1]
    done = len(refs) // 2
    copies = [pltpu.make_async_copy(refs[k], refs[done + k], sems.at[k]) for k in range(done)]
    for one in copies:
        one.start()
    for one in copies:
        one.wait()


def shards(owners, inputs, deltas, rates, skips, writer, reader, grad_out, parents, levels):
    heads = deltas.shape[1]
    columns = inputs.shape[2]
    rows = LENGTH // owners
    half = N // 2
    vm = pltpu.VMEM
    wide_b = lambda: vm((LENGTH, columns), BF16)
    wide_f = lambda: vm((LENGTH, columns), F32)
    sem = lambda n: pltpu.SemaphoreType.DMA((n,))
    anywhere = pl.BlockSpec(memory_space=pltpu.HBM)
    vectors = pl.BlockSpec(memory_space=pltpu.VMEM)
    results = (
        jax.ShapeDtypeStruct(inputs.shape, BF16),
        jax.ShapeDtypeStruct(inputs.shape, BF16),
        jax.ShapeDtypeStruct(deltas.shape, F32),
        jax.ShapeDtypeStruct((1, rows, writer.shape[2]), BF16),
        jax.ShapeDtypeStruct((1, rows, writer.shape[2]), BF16),
    )
    made = pl.pallas_call(
        functools.partial(kernel, heads, owners, 256),
        out_shape=results,
        in_specs=[anywhere] * 8,
        out_specs=[vectors] * 5,
        scratch_shapes=[
            vm((heads, LENGTH), F32), wide_b(), wide_b(), vm((LENGTH, N), BF16), vm((LENGTH, N), BF16),
            wide_b(), wide_b(), wide_b(), wide_b(), wide_b(), wide_b(), wide_b(), wide_f(), wide_f(), wide_f(), wide_f(),
            vm((N, columns), BF16), vm((N, columns), BF16), vm((SEGS // 2, 1, N), F32),
            vm((SEGS + 1, half, N), BF16), vm((SEGS + 1, half, N), BF16), vm((SEGS + 1, 1, N), F32),
            vm((SEGS + 1, half, N), F32), vm((SEGS, half, N), BF16), vm((SEGS, half, N), BF16),
            vm((N, columns), BF16), vm((N, columns), BF16), vm((SEGS // 2, 1, N), F32),
            vm((LENGTH, N), F32), vm((LENGTH, N), F32), vm((LENGTH, N), BF16), vm((owners, rows, N), F32), vm((owners, rows, N), BF16),
            pltpu.SMEM((SEGS,), jnp.int32), pltpu.SMEM((heads,), F32), pltpu.SMEM((heads,), F32),
            pltpu.SMEM((KIDS * SEGS,), jnp.int32), pltpu.SMEM((SEGS,), jnp.int32), pltpu.SMEM((SEGS,), jnp.int32),
            sem(8),
        ] + [sem(SEGS)] * 10 + [sem(owners)] * 4,
        compiler_params=pltpu.CompilerParams(
            collective_id=0, has_side_effects=True, vmem_limit_bytes=48 * 1024 * 1024
        ),
        name="tree_scan",
    )(*(pltpu.with_memory_space_constraint(a, pltpu.HBM) for a in (parents, rates, skips, deltas, inputs, grad_out, writer, reader)))
    return tuple(
        pl.pallas_call(
            store,
            out_shape=results,
            in_specs=[vectors] * 5,
            out_specs=[anywhere] * 5,
            scratch_shapes=[sem(5)],
            compiler_params=pltpu.CompilerParams(vmem_limit_bytes=32 * 1024 * 1024),
            name="store",
        )(*made)
    )


def solution(mesh):
    placed = (
        P("seg", None, "head"),
        P("seg", "head", None),
        P("head"),
        P("head"),
        P("seg", None, None),
        P("seg", None, None),
        P("seg", None, "head"),
        P(),
        P(),
    )
    return jax.shard_map(
        functools.partial(shards, mesh.shape["head"]),
        mesh=mesh,
        in_specs=placed,
        out_specs=(
            P("seg", None, "head"),
            P("seg", None, "head"),
            P("seg", "head", None),
            P("seg", "head", None),
            P("seg", "head", None),
        ),
        check_vma=False,
    )
```
